32 devices in a mesh: space: 16 (over z, y, core), bead: 2 (over x).
Axes of the slice: x: 2, y: 2, z: 4, core: 2. Of those that a mesh axis runs over, the one named last changes fastest.
Arguments:
- centroids: float32 [3, 4096], P(None, 'space'), may hold values from 0 to 1
- offsets: float32 [3, 8, 4096], P(None, 'bead', 'space'), may hold values from -1 to 1
- velocities: float32 [3, 8, 4096], P(None, 'bead', 'space'), may hold values from -12 to 12
- charges: float32 [4096], P('space'), may hold values from -3 to 3
- polar: float32 [4096], P('space'), may hold values from 0.4 to 1.6
- masses: float32 [4096], P('space'), may hold values from 1 to 16
- groups: int32 [4096], P('space'), may hold values from 0 to 2047, never falling along the last dimension, each value on 1 to 3 neighbouring positions
- tiles: int32 [32, 4], P('space'), may hold values from 0 to 5, as said below
Outputs:
- dipoles: float32 [3, 8, 4096], P(None, 'bead', 'space')
- forces: float32 [3, 8, 4096], P(None, 'bead', 'space')
- new_velocity: float32 [3, 8, 4096], P(None, 'bead', 'space')
- new_offset: float32 [3, 8, 4096], P(None, 'bead', 'space')
The draws below stay inside these ranges and needn't reach their ends.
Inputs may be any that keep to these rules, and one draw needn't show every extreme that they name: `tiles`: row c lists 4 different blocks, numbered within the concatenation of the slab before block c's slab (periodically), block c's own slab and the slab after, each of 2 blocks of 128 consecutive atoms.
All inputs are finite; a program needn't handle non-finite values.
Results may differ from the reference program's by a relative error of at most 0.0004.
Values sent between devices are 32-bit elements; how exact they have to be, the bound alone decides.
A program may use at most 64 MiB of HBM per device.

```python
import math
import jax
import jax.numpy as jnp
import numpy as np
from jax import lax

BLOCK = 128
ATOM_DEV = 256
NT = 4
ITERS = 3
BLK_DEV = 2
ATOMS = 4096
BLOCKS = 32
BEADS = 8
N_SPACE = 16


def draw_velocities(key, part):
    atom = jnp.arange(ATOMS, dtype=jnp.float32) / ATOMS
    bead = jnp.arange(BEADS, dtype=jnp.float32) / BEADS
    raw = jnp.clip(jax.random.normal(key, (3, BEADS, ATOMS), jnp.float32), -4.0, 4.0)
    spread = (1.0 + 2.0 * atom)[None, None, :] * (1.0 + 2.0 * bead)[None, :, None]
    return raw * jnp.sqrt(spread)


def draw_tiles(key, part):
    width = 3 * BLK_DEV
    scores = jax.random.randint(key, (BLOCKS, width), 0, 1 << 20) * width + jnp.arange(width, dtype=jnp.int32)[None, :]
    order = jnp.argsort(scores, axis=1, stable=True)
    return order[:, :NT].astype(jnp.int32)


def steps_of(stream_key, extent, cuts, low, top_value):
    factor_of = 1.0
    for dim, parts in cuts:
        draws = jax.random.uniform(jax.random.fold_in(jax.random.fold_in(stream_key, 6), dim), (parts,), jnp.float32, low / len(cuts), top_value / len(cuts))
        factor_of = factor_of * jnp.repeat(jnp.exp(draws), extent[dim] // parts).reshape((-1,) + (1,) * (len(extent) - 1 - dim))
    return factor_of


def profile(count, total, limit, skew):
    loads = [(1 << 20) // math.isqrt(rank ** skew) + 1 for rank in range(2, count + 1)]
    rest, counts = total - limit - (count - 1), [1] * (count - 1)
    while rest > 0:
        free = [i for i in range(count - 1) if counts[i] < limit]
        whole, left = sum([loads[i] for i in free]), rest
        for i in free:
            addition = min(limit - counts[i], max(1, left * loads[i] // whole), rest)
            counts[i] = counts[i] + addition
            rest = rest - addition
    return np.array([limit] + counts)


def uneven_parts(own_key, number_of, total, bound, lean):
    if number_of == 2:
        one = jax.random.randint(own_key, (), max(1, total - bound), min(bound, total - 1) + 1)
        return jnp.stack([one, total - one])
    tallies = jnp.asarray(profile(number_of, total, bound, lean), jnp.int32)
    couples = (number_of - 1) // 2
    source_of, sink = tallies[1:1 + 2 * couples:2], tallies[2:2 + 2 * couples:2]
    margin = jnp.minimum(source_of - 1, bound - sink)
    shifted = jax.random.randint(jax.random.fold_in(own_key, 1), (couples,), 0, 1 << 20) % (margin + 1)
    tallies = tallies.at[1:1 + 2 * couples:2].set(source_of - shifted).at[2:2 + 2 * couples:2].set(sink + shifted)
    return tallies[jax.random.permutation(jax.random.fold_in(own_key, 2), number_of)]


def normal_values(rng, extent, scale, most, cuts=(), held_as=jnp.bfloat16):
    gain = steps_of(rng, extent, cuts, -0.22, 0.18) if cuts else 1.0
    drawn = jax.random.normal(rng, extent, jnp.float32) * scale * gain
    return jnp.minimum(jnp.maximum(drawn, -most), most).astype(held_as)


def setup_inputs(seed: int = 0) -> dict:
    streams_of = jax.random.split(jax.random.key(seed), 9)
    centroids = jnp.clip(1.0 * jax.random.uniform(streams_of[0], (3, ATOMS), jnp.float32) ** steps_of(streams_of[0], (3, ATOMS), ((1, 16),), -0.2, 0.2), 0.0, 1.0)
    offsets = normal_values(streams_of[1], (3, BEADS, ATOMS), 0.2, 1.0, ((1, 2), (2, 16)), jnp.float32)
    velocities = draw_velocities(jax.random.fold_in(streams_of[8], 71), 0)
    charges = normal_values(streams_of[3], (ATOMS,), 0.5, 3.0, ((0, 16),), jnp.float32)
    polar = jnp.clip(jnp.exp(math.log(1.6) - 1.3862944 * jax.random.uniform(streams_of[4], (ATOMS,), jnp.float32) ** steps_of(streams_of[4], (ATOMS,), ((0, 16),), -0.2, 0.2)), 0.4, 1.6)
    masses = jnp.clip(jnp.exp(math.log(16.0) - 2.7725887 * jax.random.uniform(streams_of[5], (ATOMS,), jnp.float32) ** steps_of(streams_of[5], (ATOMS,), ((0, 16),), -0.2, 0.2)), 1.0, 16.0)
    groups = jnp.searchsorted(jnp.cumsum(uneven_parts(streams_of[6], ATOMS // 2, ATOMS, 3, 0)), jnp.arange(ATOMS), side="right").astype(jnp.int32)
    tiles = draw_tiles(jax.random.fold_in(streams_of[8], 71), 0)
    return {"centroids": centroids, "offsets": offsets, "velocities": velocities, "charges": charges, "polar": polar, "masses": masses, "groups": groups, "tiles": tiles}


slab_width = 9.0
box_side = 24.0
cut_square = 64.0
thole_coef = 0.39
bond_coef = 4.0
time_step = 0.05
target_temp = 8.0
coupling = 0.5

def geometry(xi, ai, gi, xj, aj, gj, keep, period):
    delta = xi[:, :, :, None] - xj[:, :, None, :]
    delta = delta - period * jnp.floor(delta / period + 0.5)
    square = lax.optimization_barrier(jnp.sum(delta * delta, axis=0)) + 1.0
    damp = thole_coef * square * jnp.sqrt(square) / jnp.sqrt(ai[:, None] * aj[None, :])
    fade = jnp.exp(-damp)
    lam_three = 1.0 - fade
    lam_five = 1.0 - (1.0 + damp) * fade
    taper = jnp.where(square < cut_square, (1.0 - square / cut_square) ** 2, 0.0)
    weight = taper * jnp.where(gi[:, None] == gj[None, :], 0.0, 1.0) * keep[None, :]
    inv_three = weight * lam_three / (square * jnp.sqrt(square))
    inv_five = 3.0 * weight * lam_five / (square * square * jnp.sqrt(square))
    return (delta, inv_three, inv_five)

def permanent(xi, ai, gi, xj, qj, aj, gj, keep, period):
    delta, inv_three, inv_five = geometry(xi, ai, gi, xj, aj, gj, keep, period)
    return lax.optimization_barrier(jnp.sum(delta * (inv_three * qj[None, :])[None], axis=-1))

def mutual(xi, ai, gi, xj, aj, gj, muj, keep, period):
    delta, inv_three, inv_five = geometry(xi, ai, gi, xj, aj, gj, keep, period)
    along = lax.optimization_barrier(jnp.sum(delta * muj[:, :, None, :], axis=0))
    return lax.optimization_barrier(jnp.sum(delta * (inv_five * along)[None], axis=-1)) - lax.optimization_barrier(jnp.sum(inv_three[None] * muj[:, :, None, :], axis=-1))

def energy(xi, xj, ai, gi, qj, aj, gj, mui, muj, keep, period):
    first = permanent(xi, ai, gi, xj, qj, aj, gj, keep, period)
    second = mutual(xi, ai, gi, xj, aj, gj, muj, keep, period)
    return -jnp.sum(mui * (first + 0.5 * second))

def reference(centroids, offsets, velocities, charges, polar, masses, groups, tiles):
    atoms = centroids.shape[1]
    beads = offsets.shape[1]
    nblocks = atoms // BLOCK
    slab_of = (jnp.arange(atoms, dtype=jnp.int32) // ATOM_DEV).astype(jnp.float32)
    base = jnp.stack([(slab_of + centroids[0]) * slab_width, centroids[1] * box_side, centroids[2] * box_side])
    positions = base[:, None, :] + offsets
    idents = groups.astype(jnp.float32)
    period = jnp.array([N_SPACE * slab_width, box_side, box_side], jnp.float32).reshape(3, 1, 1, 1)
    owner = jnp.arange(nblocks, dtype=jnp.int32) // BLK_DEV
    sources = ((owner[:, None] * BLK_DEV + tiles - BLK_DEV) % nblocks).astype(jnp.int32)
    keep = jnp.ones((NT * BLOCK,), jnp.float32)
    pos_b = positions.reshape(3, beads, nblocks, BLOCK)
    q_b = charges.reshape(nblocks, BLOCK)
    a_b = polar.reshape(nblocks, BLOCK)
    g_b = idents.reshape(nblocks, BLOCK)
    order = jnp.arange(nblocks, dtype=jnp.int32)

    def spread(field):
        return jnp.moveaxis(field, 0, 2).reshape(3, beads, atoms)

    def perm_block(c):
        src = sources[c]
        return permanent(pos_b[:, :, c], a_b[c], g_b[c], pos_b[:, :, src].reshape(3, beads, -1), q_b[src].reshape(-1), a_b[src].reshape(-1), g_b[src].reshape(-1), keep, period)
    field0 = spread(lax.map(perm_block, order))

    def mutual_field(mu):
        mu_b = mu.reshape(3, beads, nblocks, BLOCK)

        def one(c):
            src = sources[c]
            return mutual(pos_b[:, :, c], a_b[c], g_b[c], pos_b[:, :, src].reshape(3, beads, -1), a_b[src].reshape(-1), g_b[src].reshape(-1), mu_b[:, :, src].reshape(3, beads, -1), keep, period)
        return spread(lax.map(one, order))
    mu = polar * field0
    for step in range(ITERS):
        mu = polar * (field0 + mutual_field(mu))
    mu_b = mu.reshape(3, beads, nblocks, BLOCK)
    slope = jax.grad(energy, argnums=(0, 1))

    def grad_block(c):
        src = sources[c]
        return slope(pos_b[:, :, c], pos_b[:, :, src].reshape(3, beads, -1), a_b[c], g_b[c], q_b[src].reshape(-1), a_b[src].reshape(-1), g_b[src].reshape(-1), mu_b[:, :, c], mu_b[:, :, src].reshape(3, beads, -1), keep, period)
    own_grad, src_grad = lax.map(grad_block, order)
    total = jnp.moveaxis(own_grad, 0, 2)
    src_grad = jnp.moveaxis(src_grad.reshape(nblocks, 3, beads, NT, BLOCK), 0, 2).reshape(3, beads, nblocks * NT, BLOCK)
    total = total.at[:, :, sources.reshape(-1)].add(src_grad)
    forces = -total.reshape(3, beads, atoms)
    kinetic = jnp.sum(masses[None, None, :] * velocities * velocities) / (3.0 * atoms * beads)
    scale = jnp.sqrt(1.0 + coupling * (target_temp / kinetic - 1.0))
    before = jnp.roll(offsets, 1, axis=1)
    after = jnp.roll(offsets, -1, axis=1)
    restoring = -bond_coef * (2.0 * offsets - before - after)
    new_velocity = scale * velocities + time_step * (forces / masses[None, None, :] + restoring)
    new_offset = offsets + time_step * new_velocity
    return (mu, forces, new_velocity, new_offset)
```

```python
import functools

import jax
import jax.numpy as jnp
from jax import lax
from jax.experimental import pallas as pl
from jax.experimental.pallas import tpu as pltpu
from jax.sharding import PartitionSpec as P

BLOCK = 128
NT = 4
ITERS = 3
GROUPS = 2
R_GEO = 16
R_MUT = 32
R_FRC = 16

slab_width = 9.0
box_side = 24.0
cut_square = 64.0
thole_coef = 0.39
bond_coef = 4.0
time_step = 0.05
target_temp = 8.0
coupling = 0.5


def spread(col, k):
    return jnp.broadcast_to(col[:, k : k + 1], (col.shape[0], BLOCK))


def fold(value):
    total = value[0:8]
    for i in range(1, value.shape[0] // 8):
        total = total + value[8 * i : 8 * i + 8]
    return total


def kernel(
    ns,
    nbd,
    cen_ref,
    off_ref,
    vel_ref,
    chg_ref,
    pol_ref,
    mass_ref,
    grp_ref,
    tiles_ref,
    mu_out,
    force_out,
    vel_out,
    off_out,
    p_own,
    p_halo,
    col_p,
    geo,
    f0,
    mu_own,
    mu_halo,
    col_m,
    col_r,
    r_own,
    r_send,
    r_recv,
    f_own,
    ob,
    k_own,
    k_recv,
    p_ss,
    p_rs,
    m_ss,
    m_rs,
    r_ss,
    r_rs,
    o_ss,
    o_rs,
    k_ss,
    k_rs,
):
    beads = off_ref.shape[1]
    nblk = off_ref.shape[2] // BLOCK
    nb = beads // GROUPS
    me = lax.axis_index("space")
    mb = lax.axis_index("bead")
    right, left = lax.rem(me + 1, ns), lax.rem(me + ns - 1, ns)
    above, below = lax.rem(mb + 1, nbd), lax.rem(mb + nbd - 1, nbd)
    partners = []
    step = 1
    while step < ns:
        partners.append({"space": me + step - 2 * step * ((me // step) % 2)})
        step *= 2
    step = 1
    while step < nbd:
        partners.append({"bead": mb + step - 2 * step * ((mb // step) % 2)})
        step *= 2

    barrier = pltpu.get_barrier_semaphore()
    everyone = [{"space": right}, {"space": left}, {"bead": above}, {"bead": below}] + partners
    for who in everyone:
        pl.semaphore_signal(barrier, inc=1, device_id=who, device_id_type=pl.DeviceIdType.MESH)

    pending = []

    def send(src, dst, ss, rs, who):
        copy = pltpu.make_async_remote_copy(
            src_ref=src,
            dst_ref=dst,
            send_sem=ss,
            recv_sem=rs,
            device_id=who,
            device_id_type=pl.DeviceIdType.MESH,
        )
        copy.start()
        pending.append(copy)
        return copy

    for b in range(nblk):
        cut = slice(b * BLOCK, (b + 1) * BLOCK)
        p_own[b, 0:beads, :] = cen_ref[0:1, cut] * slab_width + off_ref[0, :, cut]
        for c in (1, 2):
            p_own[b, c * beads : (c + 1) * beads, :] = cen_ref[c : c + 1, cut] + off_ref[
                c, :, cut
            ] * (1.0 / box_side)
        base = 3 * beads
        p_own[b, base : base + 1, :] = chg_ref[0:1, cut]
        p_own[b, base + 1 : base + 2, :] = lax.rsqrt(pol_ref[0:1, cut])
        p_own[b, base + 2 : base + 3, :] = grp_ref[0:1, cut].astype(jnp.float32)
        p_own[b, base + 3 : base + 4, :] = pol_ref[0:1, cut]
    heat = jnp.zeros((beads, off_ref.shape[2]), jnp.float32)
    for c in range(3):
        heat = heat + vel_ref[c] * vel_ref[c]
    heat = heat * mass_ref[0:1, :]
    tally = heat[:, 0:BLOCK]
    for b in range(1, nblk):
        tally = tally + heat[:, b * BLOCK : (b + 1) * BLOCK]
    k_own[0] = jnp.zeros((8, BLOCK), jnp.float32)
    k_own[0, 0:beads, :] = tally
    for g in range(GROUPS):
        for s in range(ITERS + 1):
            mu_own[g, s] = jnp.zeros(mu_own.shape[2:], jnp.float32)

    pl.semaphore_wait(barrier, len(everyone))

    to_right = send(p_own, p_halo.at[0], p_ss.at[0], p_rs.at[0], {"space": right})
    to_left = send(p_own, p_halo.at[1], p_ss.at[1], p_rs.at[1], {"space": left})
    bead_up = send(off_ref, ob.at[0], o_ss.at[0], o_rs.at[0], {"bead": above})
    bead_down = send(off_ref, ob.at[1], o_ss.at[1], o_rs.at[1], {"bead": below})

    heat_state = {"stage": 0, "copy": None}

    def heat_send():
        s = heat_state["stage"]
        heat_state["copy"] = send(
            k_own.at[s], k_recv.at[s], k_ss.at[s], k_rs.at[s], partners[s]
        )

    def heat_step():
        s = heat_state["stage"]
        if s >= len(partners):
            return
        heat_state["copy"].wait_recv()
        k_own[s + 1] = k_own[s] + k_recv[s]
        heat_state["stage"] = s + 1
        if s + 1 < len(partners):
            heat_send()

    heat_send()

    for b in range(nblk):
        col_p[nblk + b] = p_own[b].T
    for d, copy in ((0, to_right), (1, to_left)):
        copy.wait_recv()
        move = -slab_width if d == 0 else slab_width
        row = lax.broadcasted_iota(jnp.int32, p_own.shape[1:], 0)
        for b in range(nblk):
            col_p[2 * d * nblk + b] = jnp.where(
                row < beads, p_halo[d, b] + move, p_halo[d, b]
            ).T
    heat_step()

    def geometry(g):
        chunks = BLOCK // R_GEO

        def block(b, none):
            own = p_own[b]
            full = (R_GEO, BLOCK)
            ki = jnp.broadcast_to(own[3 * beads + 1 : 3 * beads + 2] * thole_coef, full)
            gi = jnp.broadcast_to(own[3 * beads + 2 : 3 * beads + 3], full)
            xi = [
                [
                    jnp.broadcast_to(own[c * beads + g * nb + k : c * beads + g * nb + k + 1], full)
                    for c in range(3)
                ]
                for k in range(nb)
            ]

            def chunk(m, accs):
                e = tiles_ref[b, m // chunks]
                start = pl.multiple_of((m % chunks) * R_GEO, R_GEO)
                col = col_p[e, pl.ds(start, R_GEO), :]
                qj = spread(col, 3 * beads)
                kk = ki * spread(col, 3 * beads + 1)
                mask = jnp.where(gi == spread(col, 3 * beads + 2), 0.0, 1.0)
                rows = pl.ds(pl.multiple_of(b * (NT * BLOCK) + m * R_GEO, R_GEO), R_GEO)
                out = []
                for k in range(nb):
                    bead = g * nb + k
                    dx = xi[k][0] - spread(col, bead)
                    dy = xi[k][1] - spread(col, beads + bead)
                    dy = (dy - jnp.floor(dy + 0.5)) * box_side
                    dz = xi[k][2] - spread(col, 2 * beads + bead)
                    dz = (dz - jnp.floor(dz + 0.5)) * box_side
                    s = dx * dx + dy * dy + dz * dz + 1.0
                    r = lax.rsqrt(s)
                    r2 = r * r
                    u = kk * (s * s * r)
                    fade = jnp.exp(-u)
                    ue = u * fade
                    l3 = 1.0 - fade
                    l5 = l3 - ue
                    t = jnp.maximum(1.0 - s * (1.0 / cut_square), 0.0)
                    tm = t * mask
                    w = tm * t
                    r3 = r2 * r
                    wr3 = w * r3
                    b3 = wr3 * l3
                    wr5 = wr3 * r2 * 3.0
                    b5 = wr5 * l5
                    slope = tm * r3 * (-2.0 / cut_square)
                    d3 = 2.0 * slope * l3 + 3.0 * (wr3 * r2) * (ue - l3)
                    d5 = r2 * (3.0 * slope * l5 + wr5 * (1.5 * u * ue - 2.5 * l5))
                    geo[0, bead, rows, :] = dx
                    geo[1, bead, rows, :] = dy
                    geo[2, bead, rows, :] = dz
                    geo[3, bead, rows, :] = b3
                    geo[4, bead, rows, :] = b5
                    geo[5, bead, rows, :] = d3
                    geo[6, bead, rows, :] = d5
                    qb = qj * b3
                    out += [
                        accs[3 * k] + fold(qb * dx),
                        accs[3 * k + 1] + fold(qb * dy),
                        accs[3 * k + 2] + fold(qb * dz),
                    ]
                return tuple(out)

            zero = jnp.zeros((8, BLOCK), jnp.float32)
            accs = lax.fori_loop(0, NT * chunks, chunk, (zero,) * (3 * nb))
            pol = own[3 * beads + 3 : 3 * beads + 4]
            for k in range(nb):
                for c in range(3):
                    field = jnp.sum(accs[3 * k + c], axis=0, keepdims=True)
                    f0[g, b, c * nb + k : c * nb + k + 1, :] = field
                    mu_own[g, 0, b, c * nb + k : c * nb + k + 1, :] = pol * field
            return none

        lax.fori_loop(0, nblk, block, 0)

    def mu_send(g, s):
        n = 2 * (g * (ITERS + 1) + s)
        return (
            send(mu_own.at[g, s], mu_halo.at[g, s, 0], m_ss.at[n], m_rs.at[n], {"space": right}),
            send(
                mu_own.at[g, s], mu_halo.at[g, s, 1], m_ss.at[n + 1], m_rs.at[n + 1], {"space": left}
            ),
        )

    def mu_columns(g, s, copies):
        for b in range(nblk):
            col_m[g, nblk + b] = mu_own[g, s, b].T
        for d in range(2):
            copies[d].wait_recv()
            for b in range(nblk):
                col_m[g, 2 * d * nblk + b] = mu_halo[g, s, d, b].T

    def mutual(g, s):
        chunks = BLOCK // R_MUT

        def block(b, none):
            def chunk(m, accs):
                e = tiles_ref[b, m // chunks]
                start = pl.multiple_of((m % chunks) * R_MUT, R_MUT)
                col = col_m[g, e, pl.ds(start, R_MUT), :]
                rows = pl.ds(pl.multiple_of(b * (NT * BLOCK) + m * R_MUT, R_MUT), R_MUT)
                out = []
                for k in range(nb):
                    bead = g * nb + k
                    mx, my, mz = (spread(col, k), spread(col, nb + k), spread(col, 2 * nb + k))
                    dx, dy, dz = (geo[0, bead, rows, :], geo[1, bead, rows, :], geo[2, bead, rows, :])
                    b3 = geo[3, bead, rows, :]
                    along = geo[4, bead, rows, :] * (dx * mx + dy * my + dz * mz)
                    out += [
                        accs[3 * k] + fold(along * dx - b3 * mx),
                        accs[3 * k + 1] + fold(along * dy - b3 * my),
                        accs[3 * k + 2] + fold(along * dz - b3 * mz),
                    ]
                return tuple(out)

            zero = jnp.zeros((8, BLOCK), jnp.float32)
            accs = lax.fori_loop(0, NT * chunks, chunk, (zero,) * (3 * nb))
            pol = p_own[b, 3 * beads + 3 : 3 * beads + 4, :]
            for k in range(nb):
                for c in range(3):
                    row = slice(c * nb + k, c * nb + k + 1)
                    field = jnp.sum(accs[3 * k + c], axis=0, keepdims=True)
                    mu_own[g, s + 1, b, row, :] = pol * (f0[g, b, row, :] + field)
            return none

        lax.fori_loop(0, nblk, block, 0)

    def force(g):
        chunks = BLOCK // R_FRC
        lane = lax.broadcasted_iota(jnp.int32, (R_FRC, BLOCK), 1)

        def block(b, none):
            own = mu_own[g, ITERS, b]
            mi = [
                [
                    jnp.broadcast_to(own[c * nb + k : c * nb + k + 1], (R_FRC, BLOCK))
                    for c in range(3)
                ]
                for k in range(nb)
            ]

            def chunk(m, accs):
                e = tiles_ref[b, m // chunks]
                start = pl.multiple_of((m % chunks) * R_FRC, R_FRC)
                col = col_m[g, e, pl.ds(start, R_FRC), :]
                qj = spread(col_p[e, pl.ds(start, R_FRC), :], 3 * beads)
                rows = pl.ds(pl.multiple_of(b * (NT * BLOCK) + m * R_FRC, R_FRC), R_FRC)
                out = []
                packed = jnp.zeros((R_FRC, BLOCK), jnp.float32)
                for k in range(nb):
                    bead = g * nb + k
                    mj = [spread(col, c * nb + k) for c in range(3)]
                    d = [geo[c, bead, rows, :] for c in range(3)]
                    b3 = geo[3, bead, rows, :]
                    half = 0.5 * geo[4, bead, rows, :]
                    a = mi[k][0] * d[0] + mi[k][1] * d[1] + mi[k][2] * d[2]
                    bb = mj[0] * d[0] + mj[1] * d[1] + mj[2] * d[2]
                    cc = mi[k][0] * mj[0] + mi[k][1] * mj[1] + mi[k][2] * mj[2]
                    lead = geo[5, bead, rows, :] * (qj * a - 0.5 * cc) + geo[6, bead, rows, :] * (
                        a * bb
                    )
                    ci = b3 * qj + half * bb
                    cj = half * a
                    for c in range(3):
                        f = d[c] * lead + ci * mi[k][c] + cj * mj[c]
                        out.append(accs[3 * k + c] + fold(f))
                        back = jnp.sum(f, axis=1, keepdims=True)
                        packed = jnp.where(lane == c * nb + k, back, packed)
                col_r[g, rows, :] = packed
                return tuple(out)

            zero = jnp.zeros((8, BLOCK), jnp.float32)
            accs = lax.fori_loop(0, NT * chunks, chunk, (zero,) * (3 * nb))
            for k in range(nb):
                for c in range(3):
                    f_own[g, b, c * nb + k : c * nb + k + 1, :] = jnp.sum(
                        accs[3 * k + c], axis=0, keepdims=True
                    )
            return none

        lax.fori_loop(0, nblk, block, 0)

        width = mu_own.shape[3]
        sums = [jnp.zeros((width, BLOCK), jnp.float32) for _ in range(3 * nblk)]
        for b in range(nblk):
            for t in range(NT):
                first = (b * NT + t) * BLOCK
                part = col_r[g, first : first + BLOCK, :].T[0:width]
                e = tiles_ref[b, t]
                for x in range(3 * nblk):
                    sums[x] = sums[x] + part * jnp.where(e == x, 1.0, 0.0)
        for b in range(nblk):
            r_send[g, 0, b] = sums[b]
            r_own[g, b] = sums[nblk + b]
            r_send[g, 1, b] = sums[2 * nblk + b]
        n = 2 * g
        return (
            send(r_send.at[g, 0], r_recv.at[g, 0], r_ss.at[n], r_rs.at[n], {"space": left}),
            send(
                r_send.at[g, 1], r_recv.at[g, 1], r_ss.at[n + 1], r_rs.at[n + 1], {"space": right}
            ),
        )

    moving = {}
    for g in range(GROUPS):
        geometry(g)
        moving[g] = mu_send(g, 0)
        heat_step()
    for s in range(ITERS):
        for g in range(GROUPS):
            mu_columns(g, s, moving[g])
            mutual(g, s)
            moving[g] = mu_send(g, s + 1)
            heat_step()
    back = {}
    for g in range(GROUPS):
        mu_columns(g, ITERS, moving[g])
        back[g] = force(g)
        heat_step()
    while heat_state["stage"] < len(partners):
        heat_step()

    bead_up.wait_recv()
    bead_down.wait_recv()
    total = jnp.sum(jnp.sum(k_own[len(partners)], axis=1, keepdims=True), axis=0, keepdims=True)
    kinetic = total / (3.0 * off_ref.shape[2] * ns * beads * nbd)
    scale = jnp.sqrt(1.0 + coupling * (target_temp / kinetic - 1.0))

    for g in range(GROUPS):
        for b in range(nblk):
            cut = slice(b * BLOCK, (b + 1) * BLOCK)
            for c in range(3):
                mu_out[c, g * nb : (g + 1) * nb, cut] = mu_own[g, ITERS, b, c * nb : (c + 1) * nb, :]
    for g in range(GROUPS):
        for copy in back[g]:
            copy.wait_recv()
        for b in range(nblk):
            cut = slice(b * BLOCK, (b + 1) * BLOCK)
            net = f_own[g, b] - (r_own[g, b] + r_recv[g, 0, b] + r_recv[g, 1, b])
            for c in range(3):
                force_out[c, g * nb : (g + 1) * nb, cut] = net[c * nb : (c + 1) * nb]
    inverse = time_step / mass_ref[0:1, :]
    for c in range(3):
        own = off_ref[c]
        before = jnp.concatenate([ob[0, c, beads - 1 : beads, :], own[: beads - 1]], axis=0)
        after = jnp.concatenate([own[1:], ob[1, c, 0:1, :]], axis=0)
        restoring = -bond_coef * (2.0 * own - before - after)
        new_velocity = scale * vel_ref[c] + (inverse * force_out[c] + time_step * restoring)
        vel_out[c] = new_velocity
        off_out[c] = own + time_step * new_velocity
    for copy in pending:
        copy.wait_send()


def per_device(ns, nbd, centroids, offsets, velocities, charges, polar, masses, groups, tiles):
    _, beads, atoms = offsets.shape
    nblk = atoms // BLOCK
    nb = beads // GROUPS
    width = -(-3 * nb // 8) * 8
    stages = (ns - 1).bit_length() + (nbd - 1).bit_length()
    vmem = pl.BlockSpec(memory_space=pltpu.VMEM)
    f32 = jnp.float32
    plane = nblk * NT * BLOCK
    dma = pltpu.SemaphoreType.DMA
    exchanges = 2 * GROUPS * (ITERS + 1)
    return pl.pallas_call(
        functools.partial(kernel, ns, nbd),
        out_shape=[jax.ShapeDtypeStruct(offsets.shape, f32)] * 4,
        in_specs=[vmem] * 7 + [pl.BlockSpec(memory_space=pltpu.SMEM)],
        out_specs=[vmem] * 4,
        scratch_shapes=[
            pltpu.VMEM((nblk, 3 * beads + 4, BLOCK), f32),
            pltpu.VMEM((2, nblk, 3 * beads + 4, BLOCK), f32),
            pltpu.VMEM((3 * nblk, BLOCK, 3 * beads + 4), f32),
            pltpu.VMEM((7, beads, plane, BLOCK), f32),
            pltpu.VMEM((GROUPS, nblk, width, BLOCK), f32),
            pltpu.VMEM((GROUPS, ITERS + 1, nblk, width, BLOCK), f32),
            pltpu.VMEM((GROUPS, ITERS + 1, 2, nblk, width, BLOCK), f32),
            pltpu.VMEM((GROUPS, 3 * nblk, BLOCK, width), f32),
            pltpu.VMEM((GROUPS, plane, BLOCK), f32),
            pltpu.VMEM((GROUPS, nblk, width, BLOCK), f32),
            pltpu.VMEM((GROUPS, 2, nblk, width, BLOCK), f32),
            pltpu.VMEM((GROUPS, 2, nblk, width, BLOCK), f32),
            pltpu.VMEM((GROUPS, nblk, width, BLOCK), f32),
            pltpu.VMEM((2,) + offsets.shape, f32),
            pltpu.VMEM((stages + 1, 8, BLOCK), f32),
            pltpu.VMEM((stages, 8, BLOCK), f32),
            dma((2,)),
            dma((2,)),
            dma((exchanges,)),
            dma((exchanges,)),
            dma((2 * GROUPS,)),
            dma((2 * GROUPS,)),
            dma((2,)),
            dma((2,)),
            dma((stages,)),
            dma((stages,)),
        ],
        compiler_params=pltpu.CompilerParams(collective_id=0, has_side_effects=True),
    )(
        centroids,
        offsets,
        velocities,
        charges.reshape(1, atoms),
        polar.reshape(1, atoms),
        masses.reshape(1, atoms),
        groups.reshape(1, atoms),
        tiles,
    )


def solution(mesh):
    ns, nbd = mesh.shape["space"], mesh.shape["bead"]
    assert ns > 4 and ns & (ns - 1) == 0 and nbd > 1 and nbd & (nbd - 1) == 0
    placed = (
        P(None, "space"),
        P(None, "bead", "space"),
        P(None, "bead", "space"),
        P("space"),
        P("space"),
        P("space"),
        P("space"),
        P("space", None),
    )
    return jax.shard_map(
        functools.partial(per_device, ns, nbd),
        mesh=mesh,
        in_specs=placed,
        out_specs=(P(None, "bead", "space"),) * 4,
        check_vma=False,
    )
```

```python
import functools

import jax
import jax.numpy as jnp
from jax import lax
from jax.experimental import pallas as pl
from jax.experimental.pallas import tpu as pltpu
from jax.sharding import PartitionSpec as P

BLOCK = 128
NT = 4
ITERS = 3
GROUPS = 2
R_GEO = 128
R_MUT = 128
R_FRC = 128

slab_width = 9.0
box_side = 24.0
cut_square = 64.0
thole_coef = 0.39
bond_coef = 4.0
time_step = 0.05
target_temp = 8.0
coupling = 0.5


def spread(col, k):
    return jnp.broadcast_to(col[:, k : k + 1], (col.shape[0], BLOCK))


def fold(value):
    total = value[0:8]
    for i in range(1, value.shape[0] // 8):
        total = total + value[8 * i : 8 * i + 8]
    return total


def kernel(
    ns,
    nbd,
    cen_ref,
    off_ref,
    vel_ref,
    chg_ref,
    pol_ref,
    mass_ref,
    grp_ref,
    tiles_ref,
    mu_out,
    force_out,
    vel_out,
    off_out,
    p_own,
    p_halo,
    col_p,
    geo,
    f0,
    mu_own,
    mu_halo,
    col_m,
    f_own,
    slot_ref,
    ob,
    k_own,
    k_recv,
    p_ss,
    p_rs,
    m_ss,
    m_rs,
    o_ss,
    o_rs,
    k_ss,
    k_rs,
):
    beads = off_ref.shape[1]
    nblk = off_ref.shape[2] // BLOCK
    nb = beads // GROUPS
    me = lax.axis_index("space")
    mb = lax.axis_index("bead")
    right, left = lax.rem(me + 1, ns), lax.rem(me + ns - 1, ns)
    above, below = lax.rem(mb + 1, nbd), lax.rem(mb + nbd - 1, nbd)
    partners = []
    step = 1
    while step < ns:
        partners.append({"space": me + step - 2 * step * ((me // step) % 2)})
        step *= 2
    step = 1
    while step < nbd:
        partners.append({"bead": mb + step - 2 * step * ((mb // step) % 2)})
        step *= 2

    barrier = pltpu.get_barrier_semaphore()
    everyone = [{"space": right}, {"space": left}, {"bead": above}, {"bead": below}] + partners
    for who in everyone:
        pl.semaphore_signal(barrier, inc=1, device_id=who, device_id_type=pl.DeviceIdType.MESH)

    pending = []

    def send(src, dst, ss, rs, who):
        copy = pltpu.make_async_remote_copy(
            src_ref=src,
            dst_ref=dst,
            send_sem=ss,
            recv_sem=rs,
            device_id=who,
            device_id_type=pl.DeviceIdType.MESH,
        )
        copy.start()
        pending.append(copy)
        return copy

    for b in range(nblk):
        cut = slice(b * BLOCK, (b + 1) * BLOCK)
        p_own[b, 0:beads, :] = cen_ref[0:1, cut] * slab_width + off_ref[0, :, cut]
        for c in (1, 2):
            p_own[b, c * beads : (c + 1) * beads, :] = cen_ref[c : c + 1, cut] + off_ref[
                c, :, cut
            ] * (1.0 / box_side)
        base = 3 * beads
        p_own[b, base : base + 1, :] = chg_ref[0:1, cut]
        p_own[b, base + 1 : base + 2, :] = lax.rsqrt(pol_ref[0:1, cut])
        p_own[b, base + 2 : base + 3, :] = grp_ref[0:1, cut].astype(jnp.float32)
        lane = lax.broadcasted_iota(jnp.int32, (1, BLOCK), 1)
        flags = jnp.zeros((1, BLOCK), jnp.float32)
        for t in range(NT):
            flags = flags + jnp.where(lane == tiles_ref[b, t], 1.0, 0.0)
            slot_ref[b, t] = tiles_ref[b, t]
        p_own[b, base + 3 : base + 4, :] = flags
        rank = 0
        others = [0] * (3 * nblk - NT)
        for e in range(3 * nblk):
            free = 1
            for t in range(NT):
                free = jnp.where(tiles_ref[b, t] == e, 0, free)
            for x in range(3 * nblk - NT):
                others[x] = others[x] + jnp.where(rank == x, free * e, 0)
            rank = rank + free
        for x in range(3 * nblk - NT):
            slot_ref[b, NT + x] = others[x]
    heat = jnp.zeros((beads, off_ref.shape[2]), jnp.float32)
    for c in range(3):
        heat = heat + vel_ref[c] * vel_ref[c]
    heat = heat * mass_ref[0:1, :]
    tally = heat[:, 0:BLOCK]
    for b in range(1, nblk):
        tally = tally + heat[:, b * BLOCK : (b + 1) * BLOCK]
    k_own[0] = jnp.zeros((8, BLOCK), jnp.float32)
    k_own[0, 0:beads, :] = tally
    for g in range(GROUPS):
        for s in range(ITERS + 1):
            mu_own[g, s] = jnp.zeros(mu_own.shape[2:], jnp.float32)

    pl.semaphore_wait(barrier, len(everyone))

    to_right = send(p_own, p_halo.at[0], p_ss.at[0], p_rs.at[0], {"space": right})
    to_left = send(p_own, p_halo.at[1], p_ss.at[1], p_rs.at[1], {"space": left})
    bead_up = send(off_ref, ob.at[0], o_ss.at[0], o_rs.at[0], {"bead": above})
    bead_down = send(off_ref, ob.at[1], o_ss.at[1], o_rs.at[1], {"bead": below})

    heat_state = {"stage": 0, "copy": None}

    def heat_send():
        s = heat_state["stage"]
        heat_state["copy"] = send(
            k_own.at[s], k_recv.at[s], k_ss.at[s], k_rs.at[s], partners[s]
        )

    def heat_step():
        s = heat_state["stage"]
        if s >= len(partners):
            return
        heat_state["copy"].wait_recv()
        k_own[s + 1] = k_own[s] + k_recv[s]
        heat_state["stage"] = s + 1
        if s + 1 < len(partners):
            heat_send()

    heat_send()

    for b in range(nblk):
        col_p[nblk + b] = p_own[b].T
    for d, copy in ((0, to_right), (1, to_left)):
        copy.wait_recv()
        move = -slab_width if d == 0 else slab_width
        row = lax.broadcasted_iota(jnp.int32, p_own.shape[1:], 0)
        for b in range(nblk):
            col_p[2 * d * nblk + b] = jnp.where(
                row < beads, p_halo[d, b] + move, p_halo[d, b]
            ).T
    heat_step()

    def geometry(g, first, last, listed):
        chunks = BLOCK // R_GEO

        def block(b, none):
            own = p_own[b]
            full = (R_GEO, BLOCK)
            ki = jnp.broadcast_to(own[3 * beads + 1 : 3 * beads + 2] * thole_coef, full)
            gi = jnp.broadcast_to(own[3 * beads + 2 : 3 * beads + 3], full)
            xi = [
                [
                    jnp.broadcast_to(own[c * beads + g * nb + k : c * beads + g * nb + k + 1], full)
                    for c in range(3)
                ]
                for k in range(nb)
            ]

            def chunk(m, accs):
                e = slot_ref[b, m // chunks]
                start = pl.multiple_of((m % chunks) * R_GEO, R_GEO)
                col = col_p[e, pl.ds(start, R_GEO), :]
                qj = spread(col, 3 * beads)
                kk = ki * spread(col, 3 * beads + 1)
                mask = jnp.where(gi == spread(col, 3 * beads + 2), 0.0, 1.0)
                rows = pl.ds(pl.multiple_of(b * (3 * nblk * BLOCK) + m * R_GEO, R_GEO), R_GEO)
                out = []
                for k in range(nb):
                    bead = g * nb + k
                    dx = xi[k][0] - spread(col, bead)
                    dy = xi[k][1] - spread(col, beads + bead)
                    dy = (dy - jnp.floor(dy + 0.5)) * box_side
                    dz = xi[k][2] - spread(col, 2 * beads + bead)
                    dz = (dz - jnp.floor(dz + 0.5)) * box_side
                    s = dx * dx + dy * dy + dz * dz + 1.0
                    r = lax.rsqrt(s)
                    r2 = r * r
                    u = kk * (s * s * r)
                    fade = jnp.exp(-u)
                    ue = u * fade
                    l3 = 1.0 - fade
                    l5 = l3 - ue
                    t = jnp.maximum(1.0 - s * (1.0 / cut_square), 0.0)
                    tm = t * mask
                    w = tm * t
                    r3 = r2 * r
                    wr3 = w * r3
                    b3 = wr3 * l3
                    wr5 = wr3 * r2 * 3.0
                    b5 = wr5 * l5
                    slope = tm * r3 * (-2.0 / cut_square)
                    d3 = 2.0 * slope * l3 + 3.0 * (wr3 * r2) * (ue - l3)
                    d5 = r2 * (3.0 * slope * l5 + wr5 * (1.5 * u * ue - 2.5 * l5))
                    geo[0, bead, rows, :] = dx
                    geo[1, bead, rows, :] = dy
                    geo[2, bead, rows, :] = dz
                    geo[3, bead, rows, :] = b3
                    geo[4, bead, rows, :] = b5
                    geo[5, bead, rows, :] = d3
                    geo[6, bead, rows, :] = d5
                    if not listed:
                        continue
                    qb = qj * b3
                    out += [
                        accs[3 * k] + fold(qb * dx),
                        accs[3 * k + 1] + fold(qb * dy),
                        accs[3 * k + 2] + fold(qb * dz),
                    ]
                return tuple(out)

            zero = jnp.zeros((8, BLOCK), jnp.float32)
            accs = lax.fori_loop(
                first * chunks, last * chunks, chunk, (zero,) * (3 * nb if listed else 0)
            )
            if not listed:
                return none
            pol = pol_ref[0:1, pl.ds(pl.multiple_of(b * BLOCK, BLOCK), BLOCK)]
            for k in range(nb):
                for c in range(3):
                    field = jnp.sum(accs[3 * k + c], axis=0, keepdims=True)
                    f0[g, b, c * nb + k : c * nb + k + 1, :] = field
                    mu_own[g, 0, b, c * nb + k : c * nb + k + 1, :] = pol * field
            return none

        lax.fori_loop(0, nblk, block, 0)

    def mu_send(g, s):
        n = 2 * (g * (ITERS + 1) + s)
        return (
            send(mu_own.at[g, s], mu_halo.at[g, s, 0], m_ss.at[n], m_rs.at[n], {"space": right}),
            send(
                mu_own.at[g, s], mu_halo.at[g, s, 1], m_ss.at[n + 1], m_rs.at[n + 1], {"space": left}
            ),
        )

    def mu_columns(g, s, copies):
        for b in range(nblk):
            col_m[g, nblk + b] = mu_own[g, s, b].T
        for d in range(2):
            copies[d].wait_recv()
            for b in range(nblk):
                col_m[g, 2 * d * nblk + b] = mu_halo[g, s, d, b].T

    def mutual(g, s):
        chunks = BLOCK // R_MUT

        def block(b, none):
            def chunk(m, accs):
                e = tiles_ref[b, m // chunks]
                start = pl.multiple_of((m % chunks) * R_MUT, R_MUT)
                col = col_m[g, e, pl.ds(start, R_MUT), :]
                rows = pl.ds(pl.multiple_of(b * (3 * nblk * BLOCK) + m * R_MUT, R_MUT), R_MUT)
                out = []
                for k in range(nb):
                    bead = g * nb + k
                    mx, my, mz = (spread(col, k), spread(col, nb + k), spread(col, 2 * nb + k))
                    dx, dy, dz = (geo[0, bead, rows, :], geo[1, bead, rows, :], geo[2, bead, rows, :])
                    b3 = geo[3, bead, rows, :]
                    along = geo[4, bead, rows, :] * (dx * mx + dy * my + dz * mz)
                    out += [
                        accs[3 * k] + fold(along * dx - b3 * mx),
                        accs[3 * k + 1] + fold(along * dy - b3 * my),
                        accs[3 * k + 2] + fold(along * dz - b3 * mz),
                    ]
                return tuple(out)

            zero = jnp.zeros((8, BLOCK), jnp.float32)
            accs = lax.fori_loop(0, NT * chunks, chunk, (zero,) * (3 * nb))
            pol = pol_ref[0:1, pl.ds(pl.multiple_of(b * BLOCK, BLOCK), BLOCK)]
            for k in range(nb):
                for c in range(3):
                    row = slice(c * nb + k, c * nb + k + 1)
                    field = jnp.sum(accs[3 * k + c], axis=0, keepdims=True)
                    mu_own[g, s + 1, b, row, :] = pol * (f0[g, b, row, :] + field)
            return none

        lax.fori_loop(0, nblk, block, 0)

    def force(g):
        chunks = BLOCK // R_FRC

        def block(b, none):
            own = mu_own[g, ITERS, b]
            charge = p_own[b, 3 * beads : 3 * beads + 1, :]
            mi = [
                [
                    jnp.broadcast_to(own[c * nb + k : c * nb + k + 1], (R_FRC, BLOCK))
                    for c in range(3)
                ]
                for k in range(nb)
            ]

            def chunk(m, accs):
                slot = m // chunks
                e = slot_ref[b, slot]
                start = pl.multiple_of((m % chunks) * R_FRC, R_FRC)
                col = col_m[g, e, pl.ds(start, R_FRC), :]
                mine = (2 - e // nblk) * nblk + b
                full = (R_FRC, BLOCK)
                given = jnp.where(slot < NT, 1.0, 0.0)
                taken = jnp.broadcast_to(
                    col_p[e, pl.ds(mine, 1), 3 * beads + 3 : 3 * beads + 4], (1, BLOCK)
                )
                qj = spread(col_p[e, pl.ds(start, R_FRC), :], 3 * beads) * given
                qi = jnp.broadcast_to(charge * taken, full)
                both = jnp.broadcast_to(taken + given, full)
                half = 0.5 * both
                rows = pl.ds(pl.multiple_of(b * (3 * nblk * BLOCK) + m * R_FRC, R_FRC), R_FRC)
                out = []
                for k in range(nb):
                    bead = g * nb + k
                    mj = [spread(col, c * nb + k) for c in range(3)]
                    d = [geo[c, bead, rows, :] for c in range(3)]
                    b3 = geo[3, bead, rows, :]
                    hb = half * geo[4, bead, rows, :]
                    a = mi[k][0] * d[0] + mi[k][1] * d[1] + mi[k][2] * d[2]
                    bb = mj[0] * d[0] + mj[1] * d[1] + mj[2] * d[2]
                    cc = mi[k][0] * mj[0] + mi[k][1] * mj[1] + mi[k][2] * mj[2]
                    lead = geo[5, bead, rows, :] * (qj * a - qi * bb - half * cc) + geo[
                        6, bead, rows, :
                    ] * (both * (a * bb))
                    ci = b3 * qj + hb * bb
                    cj = hb * a - b3 * qi
                    for c in range(3):
                        f = d[c] * lead + ci * mi[k][c] + cj * mj[c]
                        out.append(accs[3 * k + c] + fold(f))
                return tuple(out)

            zero = jnp.zeros((8, BLOCK), jnp.float32)
            accs = lax.fori_loop(0, 3 * nblk * chunks, chunk, (zero,) * (3 * nb))
            for k in range(nb):
                for c in range(3):
                    f_own[g, b, c * nb + k : c * nb + k + 1, :] = jnp.sum(
                        accs[3 * k + c], axis=0, keepdims=True
                    )
            return none

        lax.fori_loop(0, nblk, block, 0)

    moving = {}
    for g in range(GROUPS):
        geometry(g, 0, NT, True)
        moving[g] = mu_send(g, 0)
        heat_step()
    for s in range(ITERS):
        for g in range(GROUPS):
            mu_columns(g, s, moving[g])
            mutual(g, s)
            moving[g] = mu_send(g, s + 1)
            heat_step()
        for g in range(s, GROUPS, ITERS):
            geometry(g, NT, 3 * nblk, False)
    for g in range(GROUPS):
        mu_columns(g, ITERS, moving[g])
        force(g)
        heat_step()
    while heat_state["stage"] < len(partners):
        heat_step()

    bead_up.wait_recv()
    bead_down.wait_recv()
    total = jnp.sum(jnp.sum(k_own[len(partners)], axis=1, keepdims=True), axis=0, keepdims=True)
    kinetic = total / (3.0 * off_ref.shape[2] * ns * beads * nbd)
    scale = jnp.sqrt(1.0 + coupling * (target_temp / kinetic - 1.0))

    for g in range(GROUPS):
        for b in range(nblk):
            cut = slice(b * BLOCK, (b + 1) * BLOCK)
            for c in range(3):
                mu_out[c, g * nb : (g + 1) * nb, cut] = mu_own[g, ITERS, b, c * nb : (c + 1) * nb, :]
    for g in range(GROUPS):
        for b in range(nblk):
            cut = slice(b * BLOCK, (b + 1) * BLOCK)
            net = f_own[g, b]
            for c in range(3):
                force_out[c, g * nb : (g + 1) * nb, cut] = net[c * nb : (c + 1) * nb]
    inverse = time_step / mass_ref[0:1, :]
    for c in range(3):
        own = off_ref[c]
        before = jnp.concatenate([ob[0, c, beads - 1 : beads, :], own[: beads - 1]], axis=0)
        after = jnp.concatenate([own[1:], ob[1, c, 0:1, :]], axis=0)
        restoring = -bond_coef * (2.0 * own - before - after)
        new_velocity = scale * vel_ref[c] + (inverse * force_out[c] + time_step * restoring)
        vel_out[c] = new_velocity
        off_out[c] = own + time_step * new_velocity
    for copy in pending:
        copy.wait_send()


def per_device(ns, nbd, centroids, offsets, velocities, charges, polar, masses, groups, tiles):
    _, beads, atoms = offsets.shape
    nblk = atoms // BLOCK
    nb = beads // GROUPS
    width = -(-3 * nb // 8) * 8
    stages = (ns - 1).bit_length() + (nbd - 1).bit_length()
    vmem = pl.BlockSpec(memory_space=pltpu.VMEM)
    f32 = jnp.float32
    plane = nblk * 3 * nblk * BLOCK
    dma = pltpu.SemaphoreType.DMA
    exchanges = 2 * GROUPS * (ITERS + 1)
    return pl.pallas_call(
        functools.partial(kernel, ns, nbd),
        out_shape=[jax.ShapeDtypeStruct(offsets.shape, f32)] * 4,
        in_specs=[vmem] * 7 + [pl.BlockSpec(memory_space=pltpu.SMEM)],
        out_specs=[vmem] * 4,
        scratch_shapes=[
            pltpu.VMEM((nblk, 3 * beads + 4, BLOCK), f32),
            pltpu.VMEM((2, nblk, 3 * beads + 4, BLOCK), f32),
            pltpu.VMEM((3 * nblk, BLOCK, 3 * beads + 4), f32),
            pltpu.VMEM((7, beads, plane, BLOCK), f32),
            pltpu.VMEM((GROUPS, nblk, width, BLOCK), f32),
            pltpu.VMEM((GROUPS, ITERS + 1, nblk, width, BLOCK), f32),
            pltpu.VMEM((GROUPS, ITERS + 1, 2, nblk, width, BLOCK), f32),
            pltpu.VMEM((GROUPS, 3 * nblk, BLOCK, width), f32),
            pltpu.VMEM((GROUPS, nblk, width, BLOCK), f32),
            pltpu.SMEM((nblk, 3 * nblk), jnp.int32),
            pltpu.VMEM((2,) + offsets.shape, f32),
            pltpu.VMEM((stages + 1, 8, BLOCK), f32),
            pltpu.VMEM((stages, 8, BLOCK), f32),
            dma((2,)),
            dma((2,)),
            dma((exchanges,)),
            dma((exchanges,)),
            dma((2,)),
            dma((2,)),
            dma((stages,)),
            dma((stages,)),
        ],
        compiler_params=pltpu.CompilerParams(collective_id=0, has_side_effects=True),
    )(
        centroids,
        offsets,
        velocities,
        charges.reshape(1, atoms),
        polar.reshape(1, atoms),
        masses.reshape(1, atoms),
        groups.reshape(1, atoms),
        tiles,
    )


def solution(mesh):
    ns, nbd = mesh.shape["space"], mesh.shape["bead"]
    assert ns > 4 and ns & (ns - 1) == 0 and nbd > 1 and nbd & (nbd - 1) == 0
    placed = (
        P(None, "space"),
        P(None, "bead", "space"),
        P(None, "bead", "space"),
        P("space"),
        P("space"),
        P("space"),
        P("space"),
        P("space", None),
    )
    return jax.shard_map(
        functools.partial(per_device, ns, nbd),
        mesh=mesh,
        in_specs=placed,
        out_specs=(P(None, "bead", "space"),) * 4,
        check_vma=False,
    )
```

```python
import functools

import jax
import jax.numpy as jnp
from jax import lax
from jax.experimental import pallas as pl
from jax.experimental.pallas import tpu as pltpu
from jax.sharding import PartitionSpec as P

BLOCK = 128
NT = 4
ITERS = 3
GROUPS = 2
R_GEO = 128
R_MUT = 128
R_FRC = 128

slab_width = 9.0
box_side = 24.0
cut_square = 64.0
thole_coef = 0.39
bond_coef = 4.0
time_step = 0.05
target_temp = 8.0
coupling = 0.5
log2_e = 1.4426950408889634


def spread(col, k):
    return jnp.broadcast_to(col[:, k : k + 1], (col.shape[0], BLOCK))


def fold(value):
    total = value[0:8]
    for i in range(1, value.shape[0] // 8):
        total = total + value[8 * i : 8 * i + 8]
    return total


def kernel(
    ns,
    nbd,
    cen_ref,
    off_ref,
    vel_ref,
    chg_ref,
    pol_ref,
    mass_ref,
    grp_ref,
    tiles_ref,
    mu_out,
    force_out,
    vel_out,
    off_out,
    p_own,
    p_halo,
    col_p,
    geo,
    f0,
    mu_own,
    mu_halo,
    wide_m,
    f_own,
    slot_ref,
    ob,
    k_own,
    k_recv,
    p_ss,
    p_rs,
    m_ss,
    m_rs,
    o_ss,
    o_rs,
    k_ss,
    k_rs,
):
    beads = off_ref.shape[1]
    nblk = off_ref.shape[2] // BLOCK
    nb = beads // GROUPS
    me = lax.axis_index("space")
    mb = lax.axis_index("bead")
    right, left = lax.rem(me + 1, ns), lax.rem(me + ns - 1, ns)
    above, below = lax.rem(mb + 1, nbd), lax.rem(mb + nbd - 1, nbd)
    partners = []
    step = 1
    while step < ns:
        partners.append({"space": me + step - 2 * step * ((me // step) % 2)})
        step *= 2
    step = 1
    while step < nbd:
        partners.append({"bead": mb + step - 2 * step * ((mb // step) % 2)})
        step *= 2

    barrier = pltpu.get_barrier_semaphore()
    everyone = [{"space": right}, {"space": left}, {"bead": above}, {"bead": below}] + partners
    for who in everyone:
        pl.semaphore_signal(barrier, inc=1, device_id=who, device_id_type=pl.DeviceIdType.MESH)

    pending = []

    def send(src, dst, ss, rs, who):
        copy = pltpu.make_async_remote_copy(
            src_ref=src,
            dst_ref=dst,
            send_sem=ss,
            recv_sem=rs,
            device_id=who,
            device_id_type=pl.DeviceIdType.MESH,
        )
        copy.start()
        pending.append(copy)
        return copy

    for b in range(nblk):
        cut = slice(b * BLOCK, (b + 1) * BLOCK)
        p_own[b, 0:beads, :] = cen_ref[0:1, cut] * slab_width + off_ref[0, :, cut]
        for c in (1, 2):
            p_own[b, c * beads : (c + 1) * beads, :] = cen_ref[c : c + 1, cut] + off_ref[
                c, :, cut
            ] * (1.0 / box_side)
        base = 3 * beads
        p_own[b, base : base + 1, :] = chg_ref[0:1, cut]
        p_own[b, base + 1 : base + 2, :] = lax.rsqrt(pol_ref[0:1, cut])
        p_own[b, base + 2 : base + 3, :] = grp_ref[0:1, cut].astype(jnp.float32)
        lane = lax.broadcasted_iota(jnp.int32, (1, BLOCK), 1)
        flags = jnp.zeros((1, BLOCK), jnp.float32)
        for t in range(NT):
            flags = flags + jnp.where(lane == tiles_ref[b, t], 1.0, 0.0)
            slot_ref[b, t] = tiles_ref[b, t]
        p_own[b, base + 3 : base + 4, :] = flags
        rank = 0
        others = [0] * (3 * nblk - NT)
        for e in range(3 * nblk):
            free = 1
            for t in range(NT):
                free = jnp.where(tiles_ref[b, t] == e, 0, free)
            for x in range(3 * nblk - NT):
                others[x] = others[x] + jnp.where(rank == x, free * e, 0)
            rank = rank + free
        for x in range(3 * nblk - NT):
            slot_ref[b, NT + x] = others[x]
    heat = jnp.zeros((beads, off_ref.shape[2]), jnp.float32)
    for c in range(3):
        heat = heat + vel_ref[c] * vel_ref[c]
    heat = heat * mass_ref[0:1, :]
    tally = heat[:, 0:BLOCK]
    for b in range(1, nblk):
        tally = tally + heat[:, b * BLOCK : (b + 1) * BLOCK]
    k_own[0] = jnp.zeros((8, BLOCK), jnp.float32)
    k_own[0, 0:beads, :] = tally
    for g in range(GROUPS):
        for s in range(ITERS + 1):
            mu_own[g, s] = jnp.zeros(mu_own.shape[2:], jnp.float32)

    pl.semaphore_wait(barrier, len(everyone))

    to_right = send(p_own, p_halo.at[0], p_ss.at[0], p_rs.at[0], {"space": right})
    to_left = send(p_own, p_halo.at[1], p_ss.at[1], p_rs.at[1], {"space": left})
    bead_up = send(off_ref, ob.at[0], o_ss.at[0], o_rs.at[0], {"bead": above})
    bead_down = send(off_ref, ob.at[1], o_ss.at[1], o_rs.at[1], {"bead": below})

    heat_state = {"stage": 0, "copy": None}

    def heat_send():
        s = heat_state["stage"]
        heat_state["copy"] = send(
            k_own.at[s], k_recv.at[s], k_ss.at[s], k_rs.at[s], partners[s]
        )

    def heat_step():
        s = heat_state["stage"]
        if s >= len(partners):
            return
        heat_state["copy"].wait_recv()
        k_own[s + 1] = k_own[s] + k_recv[s]
        heat_state["stage"] = s + 1
        if s + 1 < len(partners):
            heat_send()

    heat_send()

    for b in range(nblk):
        col_p[nblk + b] = p_own[b].T
    for d, copy in ((0, to_right), (1, to_left)):
        copy.wait_recv()
        move = -slab_width if d == 0 else slab_width
        row = lax.broadcasted_iota(jnp.int32, p_own.shape[1:], 0)
        for b in range(nblk):
            col_p[2 * d * nblk + b] = jnp.where(
                row < beads, p_halo[d, b] + move, p_halo[d, b]
            ).T
    heat_step()

    def geometry(g, first, last, listed, start, stop):
        chunks = BLOCK // R_GEO

        def block(b, none):
            own = p_own[b]
            full = (R_GEO, BLOCK)
            ki = jnp.broadcast_to(own[3 * beads + 1 : 3 * beads + 2] * thole_coef, full)
            gi = jnp.broadcast_to(own[3 * beads + 2 : 3 * beads + 3], full)
            xi = [
                [
                    jnp.broadcast_to(own[c * beads + g * nb + k : c * beads + g * nb + k + 1], full)
                    for c in range(3)
                ]
                for k in range(nb)
            ]

            def chunk(m, accs):
                e = slot_ref[b, m // chunks]
                low = pl.multiple_of((m % chunks) * R_GEO, R_GEO)
                col = col_p[e, pl.ds(low, R_GEO), :]
                qj = spread(col, 3 * beads)
                kk = ki * spread(col, 3 * beads + 1)
                mask = jnp.where(gi == spread(col, 3 * beads + 2), 0.0, cut_square**-2)
                rows = pl.ds(pl.multiple_of(b * (3 * nblk * BLOCK) + m * R_GEO, R_GEO), R_GEO)
                out = []
                for k in range(nb):
                    bead = g * nb + k
                    dx = xi[k][0] - spread(col, bead)
                    dy = xi[k][1] - spread(col, beads + bead)
                    dy = (dy - jnp.floor(dy + 0.5)) * box_side
                    dz = xi[k][2] - spread(col, 2 * beads + bead)
                    dz = (dz - jnp.floor(dz + 0.5)) * box_side
                    s = dx * dx + dy * dy + dz * dz + 1.0
                    r = lax.rsqrt(s)
                    r2 = r * r
                    u = kk * (s * s * r)
                    fade = jnp.exp2(u * -log2_e)
                    ue = u * fade
                    l3 = 1.0 - fade
                    l5 = l3 - ue
                    t = jnp.maximum(cut_square - s, 0.0)
                    p = t * mask * (r2 * r)
                    wr3 = p * t
                    b3 = wr3 * l3
                    h3 = 3.0 * (wr3 * r2)
                    b5 = h3 * l5
                    p4 = -4.0 * p
                    d3 = p4 * l3 - b5
                    d5 = r2 * (p4 * l5 + h3 * (u * ue) - (5.0 / 3.0) * b5)
                    geo[0, bead, rows, :] = dx
                    geo[1, bead, rows, :] = dy
                    geo[2, bead, rows, :] = dz
                    geo[3, bead, rows, :] = b3
                    geo[4, bead, rows, :] = b5
                    geo[5, bead, rows, :] = d3
                    geo[6, bead, rows, :] = d5
                    if not listed:
                        continue
                    qb = qj * b3
                    out += [
                        accs[3 * k] + fold(qb * dx),
                        accs[3 * k + 1] + fold(qb * dy),
                        accs[3 * k + 2] + fold(qb * dz),
                    ]
                return tuple(out)

            zero = jnp.zeros((8, BLOCK), jnp.float32)
            accs = lax.fori_loop(
                first * chunks, last * chunks, chunk, (zero,) * (3 * nb if listed else 0)
            )
            if not listed:
                return none
            pol = pol_ref[0:1, pl.ds(pl.multiple_of(b * BLOCK, BLOCK), BLOCK)]
            for k in range(nb):
                for c in range(3):
                    field = jnp.sum(accs[3 * k + c], axis=0, keepdims=True)
                    f0[g, b, c * nb + k : c * nb + k + 1, :] = field
                    mu_own[g, 0, b, c * nb + k : c * nb + k + 1, :] = pol * field
            return none

        lax.fori_loop(start, stop, block, 0)

    def mu_send(g, s):
        n = 2 * (g * (ITERS + 1) + s)
        return (
            send(mu_own.at[g, s], mu_halo.at[g, s, 0], m_ss.at[n], m_rs.at[n], {"space": right}),
            send(
                mu_own.at[g, s], mu_halo.at[g, s, 1], m_ss.at[n + 1], m_rs.at[n + 1], {"space": left}
            ),
        )

    def widen(g, e, rows):
        col = rows.T
        for k in range(3 * nb):
            wide_m[g, e, k] = spread(col, k)

    def mu_columns(g, s, copies):
        for b in range(nblk):
            widen(g, nblk + b, mu_own[g, s, b])
        for d in range(2):
            copies[d].wait_recv()
            for b in range(nblk):
                widen(g, 2 * d * nblk + b, mu_halo[g, s, d, b])

    def mutual(g, s):
        chunks = BLOCK // R_MUT

        def block(b, none):
            def chunk(m, accs):
                e = tiles_ref[b, m // chunks]
                start = pl.multiple_of((m % chunks) * R_MUT, R_MUT)
                rows = pl.ds(pl.multiple_of(b * (3 * nblk * BLOCK) + m * R_MUT, R_MUT), R_MUT)
                out = []
                for k in range(nb):
                    bead = g * nb + k
                    mx, my, mz = (wide_m[g, e, c * nb + k, pl.ds(start, R_MUT), :] for c in range(3))
                    dx, dy, dz = (geo[0, bead, rows, :], geo[1, bead, rows, :], geo[2, bead, rows, :])
                    b3 = geo[3, bead, rows, :]
                    along = geo[4, bead, rows, :] * (dx * mx + dy * my + dz * mz)
                    out += [
                        accs[3 * k] + fold(along * dx - b3 * mx),
                        accs[3 * k + 1] + fold(along * dy - b3 * my),
                        accs[3 * k + 2] + fold(along * dz - b3 * mz),
                    ]
                return tuple(out)

            zero = jnp.zeros((8, BLOCK), jnp.float32)
            accs = lax.fori_loop(0, NT * chunks, chunk, (zero,) * (3 * nb))
            pol = pol_ref[0:1, pl.ds(pl.multiple_of(b * BLOCK, BLOCK), BLOCK)]
            for k in range(nb):
                for c in range(3):
                    row = slice(c * nb + k, c * nb + k + 1)
                    field = jnp.sum(accs[3 * k + c], axis=0, keepdims=True)
                    mu_own[g, s + 1, b, row, :] = pol * (f0[g, b, row, :] + field)
            return none

        lax.fori_loop(0, nblk, block, 0)

    def force(g):
        chunks = BLOCK // R_FRC

        def block(b, none):
            own = mu_own[g, ITERS, b]
            charge = p_own[b, 3 * beads : 3 * beads + 1, :]
            mi = [
                [
                    jnp.broadcast_to(own[c * nb + k : c * nb + k + 1], (R_FRC, BLOCK))
                    for c in range(3)
                ]
                for k in range(nb)
            ]

            def chunk(m, accs):
                slot = m // chunks
                e = slot_ref[b, slot]
                start = pl.multiple_of((m % chunks) * R_FRC, R_FRC)
                mine = (2 - e // nblk) * nblk + b
                full = (R_FRC, BLOCK)
                given = jnp.where(slot < NT, 1.0, 0.0)
                taken = jnp.broadcast_to(
                    col_p[e, pl.ds(mine, 1), 3 * beads + 3 : 3 * beads + 4], (1, BLOCK)
                )
                qj = spread(col_p[e, pl.ds(start, R_FRC), :], 3 * beads) * given
                qi = jnp.broadcast_to(charge * taken, full)
                both = jnp.broadcast_to(taken + given, full)
                half = 0.5 * both
                steep = 1.5 * both
                rows = pl.ds(pl.multiple_of(b * (3 * nblk * BLOCK) + m * R_FRC, R_FRC), R_FRC)
                out = []
                for k in range(nb):
                    bead = g * nb + k
                    mj = [wide_m[g, e, c * nb + k, pl.ds(start, R_FRC), :] for c in range(3)]
                    d = [geo[c, bead, rows, :] for c in range(3)]
                    b3 = geo[3, bead, rows, :]
                    hb = half * geo[4, bead, rows, :]
                    a = mi[k][0] * d[0] + mi[k][1] * d[1] + mi[k][2] * d[2]
                    bb = mj[0] * d[0] + mj[1] * d[1] + mj[2] * d[2]
                    cc = mi[k][0] * mj[0] + mi[k][1] * mj[1] + mi[k][2] * mj[2]
                    lead = geo[5, bead, rows, :] * (qj * a - qi * bb - half * cc) + geo[
                        6, bead, rows, :
                    ] * (steep * (a * bb))
                    ci = b3 * qj + hb * bb
                    cj = hb * a - b3 * qi
                    for c in range(3):
                        f = d[c] * lead + ci * mi[k][c] + cj * mj[c]
                        out.append(accs[3 * k + c] + fold(f))
                return tuple(out)

            zero = jnp.zeros((8, BLOCK), jnp.float32)
            accs = lax.fori_loop(0, 3 * nblk * chunks, chunk, (zero,) * (3 * nb))
            for k in range(nb):
                for c in range(3):
                    f_own[g, b, c * nb + k : c * nb + k + 1, :] = jnp.sum(
                        accs[3 * k + c], axis=0, keepdims=True
                    )
            return none

        lax.fori_loop(0, nblk, block, 0)

    rest = [(g, b) for g in range(GROUPS) for b in range(nblk)]

    def fill():
        if rest:
            g, b = rest.pop(0)
            geometry(g, NT, 3 * nblk, False, b, b + 1)

    moving = {}
    for g in range(GROUPS):
        geometry(g, 0, NT, True, 0, nblk)
        moving[g] = mu_send(g, 0)
        heat_step()
    fill()
    for s in range(ITERS):
        for g in range(GROUPS):
            mu_columns(g, s, moving[g])
            mutual(g, s)
            moving[g] = mu_send(g, s + 1)
            heat_step()
        fill()
    while rest:
        fill()
    for g in range(GROUPS):
        mu_columns(g, ITERS, moving[g])
        force(g)
        heat_step()
    while heat_state["stage"] < len(partners):
        heat_step()

    bead_up.wait_recv()
    bead_down.wait_recv()
    total = jnp.sum(jnp.sum(k_own[len(partners)], axis=1, keepdims=True), axis=0, keepdims=True)
    kinetic = total / (3.0 * off_ref.shape[2] * ns * beads * nbd)
    scale = jnp.sqrt(1.0 + coupling * (target_temp / kinetic - 1.0))

    for g in range(GROUPS):
        for b in range(nblk):
            cut = slice(b * BLOCK, (b + 1) * BLOCK)
            for c in range(3):
                mu_out[c, g * nb : (g + 1) * nb, cut] = mu_own[g, ITERS, b, c * nb : (c + 1) * nb, :]
    for g in range(GROUPS):
        for b in range(nblk):
            cut = slice(b * BLOCK, (b + 1) * BLOCK)
            net = f_own[g, b]
            for c in range(3):
                force_out[c, g * nb : (g + 1) * nb, cut] = net[c * nb : (c + 1) * nb]
    inverse = time_step / mass_ref[0:1, :]
    for c in range(3):
        own = off_ref[c]
        before = jnp.concatenate([ob[0, c, beads - 1 : beads, :], own[: beads - 1]], axis=0)
        after = jnp.concatenate([own[1:], ob[1, c, 0:1, :]], axis=0)
        restoring = -bond_coef * (2.0 * own - before - after)
        new_velocity = scale * vel_ref[c] + (inverse * force_out[c] + time_step * restoring)
        vel_out[c] = new_velocity
        off_out[c] = own + time_step * new_velocity
    for copy in pending:
        copy.wait_send()


def relay(*refs):
    count = (len(refs) - 1) // 2
    copies = [
        pltpu.make_async_copy(refs[i], refs[count + i], refs[-1].at[i]) for i in range(count)
    ]
    for copy in copies:
        copy.start()
    for copy in copies:
        copy.wait()


def per_device(ns, nbd, centroids, offsets, velocities, charges, polar, masses, groups, tiles):
    _, beads, atoms = offsets.shape
    nblk = atoms // BLOCK
    nb = beads // GROUPS
    width = -(-3 * nb // 8) * 8
    stages = (ns - 1).bit_length() + (nbd - 1).bit_length()
    vmem = pl.BlockSpec(memory_space=pltpu.VMEM)
    f32 = jnp.float32
    plane = nblk * 3 * nblk * BLOCK
    dma = pltpu.SemaphoreType.DMA
    exchanges = 2 * GROUPS * (ITERS + 1)
    results = pl.pallas_call(
        functools.partial(kernel, ns, nbd),
        out_shape=[jax.ShapeDtypeStruct(offsets.shape, f32)] * 4,
        in_specs=[vmem] * 7 + [pl.BlockSpec(memory_space=pltpu.SMEM)],
        out_specs=[vmem] * 4,
        scratch_shapes=[
            pltpu.VMEM((nblk, 3 * beads + 4, BLOCK), f32),
            pltpu.VMEM((2, nblk, 3 * beads + 4, BLOCK), f32),
            pltpu.VMEM((3 * nblk, BLOCK, 3 * beads + 4), f32),
            pltpu.VMEM((7, beads, plane, BLOCK), f32),
            pltpu.VMEM((GROUPS, nblk, width, BLOCK), f32),
            pltpu.VMEM((GROUPS, ITERS + 1, nblk, width, BLOCK), f32),
            pltpu.VMEM((GROUPS, ITERS + 1, 2, nblk, width, BLOCK), f32),
            pltpu.VMEM((GROUPS, 3 * nblk, 3 * nb, BLOCK, BLOCK), f32),
            pltpu.VMEM((GROUPS, nblk, width, BLOCK), f32),
            pltpu.SMEM((nblk, 3 * nblk), jnp.int32),
            pltpu.VMEM((2,) + offsets.shape, f32),
            pltpu.VMEM((stages + 1, 8, BLOCK), f32),
            pltpu.VMEM((stages, 8, BLOCK), f32),
            dma((2,)),
            dma((2,)),
            dma((exchanges,)),
            dma((exchanges,)),
            dma((2,)),
            dma((2,)),
            dma((stages,)),
            dma((stages,)),
        ],
        compiler_params=pltpu.CompilerParams(collective_id=0, has_side_effects=True),
    )(
        centroids,
        offsets,
        velocities,
        charges.reshape(1, atoms),
        polar.reshape(1, atoms),
        masses.reshape(1, atoms),
        groups.reshape(1, atoms),
        tiles,
    )
    anywhere = pl.BlockSpec(memory_space=pl.ANY)
    return pl.pallas_call(
        relay,
        out_shape=[jax.ShapeDtypeStruct(offsets.shape, f32)] * 4,
        in_specs=[anywhere] * 4,
        out_specs=[anywhere] * 4,
        scratch_shapes=[dma((4,))],
    )(*results)


def solution(mesh):
    ns, nbd = mesh.shape["space"], mesh.shape["bead"]
    assert ns > 4 and ns & (ns - 1) == 0 and nbd > 1 and nbd & (nbd - 1) == 0
    placed = (
        P(None, "space"),
        P(None, "bead", "space"),
        P(None, "bead", "space"),
        P("space"),
        P("space"),
        P("space"),
        P("space"),
        P("space", None),
    )
    return jax.shard_map(
        functools.partial(per_device, ns, nbd),
        mesh=mesh,
        in_specs=placed,
        out_specs=(P(None, "bead", "space"),) * 4,
        check_vma=False,
    )
```
